128 devices in a mesh: feat: 8 (over x_lo, y), dp: 16 (over z, x_hi, core).
Axes of the slice: x: 4 (x_hi: 2, x_lo: 2; x = x_hi * 2 + x_lo), y: 4, z: 4, core: 2. Of those that a mesh axis runs over, the one named last changes fastest.
Arguments:
- text_rows: bfloat16 [2048, 8192], P('dp', 'feat'), may hold values from -6 to 6
- q_weight: bfloat16 [8192, 8192], P(None, 'feat'), may hold values from -0.0625 to 0.0625
- features: bfloat16 [16, 1024, 7680], P('dp', None, 'feat'), may hold values from -6 to 6
- kv_weight: bfloat16 [7680, 2048], P('feat'), may hold values from -0.0625 to 0.0625
- q_gain: float32 [128], replicated, may hold values from 0.7 to 2.6
- k_gain: float32 [128], replicated, may hold values from 0.7 to 2.6
- attn_gate: float32 [1], replicated, may hold values from 0.5 to 2
- image_ids: int32 [256, 2], P('dp'), may hold values from 0 to 15, all different within a row; in each aligned block of 16 rows (0 to 15, 16 to 31, ...) at most 4 rows name the same one
- image_slot: int32 [16], replicated, may hold values from 0 to 15, each once
Outputs:
- attended: bfloat16 [2048, 8192], P('dp', 'feat')
The draws below stay inside these ranges and needn't reach their ends.
Inputs may be any that keep to these rules, and one draw needn't show every extreme that they name: `image_ids`: each request names two different images; among the requests of one index of dp (aligned blocks of 16 requests) no image is named more than 4 times, a bound that some block reaches. Each position once; image i lies at position image_slot[i].
All inputs are finite; a program needn't handle non-finite values.
Results may differ from the reference program's by a relative error of at most 0.009.
The reference program's roundings to bfloat16 on the way count: a program that leaves them out, or rounds other values in their place, can miss the bound.
Values may be sent and summed in bfloat16 or wider, within the bound.
No kernel may reach another device: no remote copies, remote signals or barrier semaphores. Data moves between devices by JAX's collectives and lax.ppermute only.
A program may use at most 128 MiB of HBM per device.

```python
import math
import jax
import jax.numpy as jnp
import numpy as np
from jax import lax

D = 8192
HEADS = 64
KVH = 8
HD = 128
FEAT = 7680
TEXT = 8
RQ_DEV = 16
VT = 1024
NIMG = 16
REQUESTS = 256
ROWS = 2048
CAP = 4


def block_scale(key, dims, split, least, top_value):
    loudness, own = 1.0, jax.random.fold_in(key, 6)
    for axis_at, shards_of in split:
        draws = jnp.exp(jax.random.uniform(jax.random.fold_in(own, axis_at), (shards_of,), jnp.float32, least / len(split), top_value / len(split)))
        loudness = loudness * jnp.repeat(draws, dims[axis_at] // shards_of).reshape([-1 if axis == axis_at else 1 for axis in range(len(dims))])
    return loudness


def deal_out(stream_key, own, number, rows, count, top, limit, lean):
    ranking = jax.random.permutation(stream_key, count)
    packed, common = load_shares(count, rows * top, limit, lean, True), load_shares(count, rows * top, limit, lean, False)
    places = jnp.arange(count)

    def named(sizes, offset_by):
        used = int((sizes > 0).sum())
        fixed = max(1, used // 4)
        passed = fixed + (places - fixed + offset_by * (used - fixed)) % max(1, count - fixed)
        return jnp.zeros((count,), jnp.int32).at[ranking[jnp.where(places < fixed, places, passed)]].set(jnp.asarray(sizes, jnp.int32))

    sizes = jnp.where(number % 4 == 0, named(packed, number // 4), named(common, number - number // 4 - 1))
    mixed = jax.random.permutation(jax.random.fold_in(own, 3), count)
    source_of, sink = mixed[0:count // 2 * 2:2], mixed[1:count // 2 * 2:2]
    slack = jnp.minimum(sizes[source_of] - 1, limit - sizes[sink]) // 2
    slack = jnp.where((source_of == ranking[0]) | (sink == ranking[0]) | (sizes[sink] == 0), 0, jnp.maximum(slack, 0))
    passed = jax.random.randint(jax.random.fold_in(own, 4), (count // 2,), 0, 1 << 20) % (slack + 1)
    sizes = sizes.at[source_of].add(-passed).at[sink].add(passed)
    members = jnp.searchsorted(jnp.cumsum(sizes), jnp.arange(rows * top), side="right").astype(jnp.int32)
    table = members.reshape(top, rows).T
    table = table[jax.random.permutation(jax.random.fold_in(own, 1), rows)]
    offset_by = jax.random.randint(jax.random.fold_in(own, 2), (rows, 1), 0, top)
    return jnp.take_along_axis(table, (jnp.arange(top)[None, :] + offset_by) % top, axis=1)


def load_shares(amount, total, most, skew, full):
    weights = [(1 << 20) // math.isqrt(rank ** skew) + 1 for rank in range(1, amount + 1)]
    largest = most if full else min(most, max(-(-total // amount), total * weights[0] // sum(weights)))
    least = 1 if total - largest >= amount - 1 else 0
    given, spare = [largest] + [least] * (amount - 1), total - largest - least * (amount - 1)
    while spare > 0:
        free = [i for i in range(1, amount) if given[i] < largest] or [i for i in range(1, amount) if given[i] < most]
        whole, left = sum([weights[i] for i in free]), spare
        for i in free:
            more = min(most - given[i], max(1, left * weights[i] // whole), spare)
            given[i] = given[i] + more
            spare = spare - more
    return np.array(given)


def scatter_about(own_key, dims, scale, bound, split=(), kind=jnp.bfloat16):
    values = jax.random.normal(own_key, dims, jnp.float32) * scale
    if len(split) > 0:
        values = block_scale(own_key, dims, split, -0.22, 0.18) * values
    return jnp.clip(values, min=-bound, max=bound).astype(kind)


def setup_inputs(seed: int = 0) -> dict:
    splits = jax.random.split(jax.random.key(seed), 10)
    text_rows = scatter_about(splits[0], (ROWS, D), 1.0, 6.0, ((0, 16), (1, 8)))
    q_weight = scatter_about(splits[1], (D, HEADS * HD), D ** -0.5, 0.0625, ((1, 8),))
    features = scatter_about(splits[2], (NIMG, VT, FEAT), 1.0, 6.0, ((0, 16), (2, 8)))
    kv_weight = scatter_about(splits[3], (FEAT, KVH * 2 * HD), FEAT ** -0.5, 0.0625, ((0, 8),))
    q_gain = jnp.clip(jnp.exp(jax.random.uniform(splits[4], (HD,), jnp.float32, math.log(0.7), math.log(2.6))), 0.7, 2.6)
    k_gain = jnp.clip(jnp.exp(jax.random.uniform(splits[5], (HD,), jnp.float32, math.log(0.7), math.log(2.6))), 0.7, 2.6)
    attn_gate = jnp.clip(jax.random.uniform(splits[6], (1,), jnp.float32, 0.5, 2.0), 0.5, 2.0)
    image_ids_keys = jax.random.split(jax.random.fold_in(splits[7], 1), REQUESTS // RQ_DEV)
    image_ids_turns = jax.random.permutation(jax.random.fold_in(splits[7], 3), REQUESTS // RQ_DEV)
    image_ids = jax.vmap(lambda own, number: deal_out(jax.random.fold_in(splits[7], 2), own, number, RQ_DEV, NIMG, 2, CAP, 2))(image_ids_keys, image_ids_turns).reshape((REQUESTS, 2))
    image_slot = jax.random.permutation(splits[8], NIMG).astype(jnp.int32)
    return dict(text_rows=text_rows, q_weight=q_weight, features=features, kv_weight=kv_weight, q_gain=q_gain, k_gain=k_gain, attn_gate=attn_gate, image_ids=image_ids, image_slot=image_slot)


epsilon = 1e-05

def head_norm(values, gain_vector):
    return values * lax.rsqrt(lax.optimization_barrier(jnp.mean(values * values, axis=-1, keepdims=True)) + epsilon) * gain_vector

def reference(text_rows, q_weight, features, kv_weight, q_gain, k_gain, attn_gate, image_ids, image_slot):
    highest = lax.Precision.HIGHEST
    group_size = HEADS // KVH
    queries = jnp.dot(text_rows.astype(jnp.float32), q_weight.astype(jnp.float32), precision=highest)
    normed = head_norm(queries.reshape(ROWS, KVH, group_size, HD), q_gain) * HD ** (-0.5)
    normed = normed.astype(jnp.bfloat16).reshape(REQUESTS, TEXT, KVH, group_size, HD)
    kv_table = kv_weight.astype(jnp.float32)

    def project(vision_rows):
        summed = jnp.dot(vision_rows.astype(jnp.float32), kv_table, precision=highest).reshape(VT, KVH, 2 * HD)
        normed_keys = head_norm(summed[..., :HD], k_gain)
        return jnp.concatenate([normed_keys, summed[..., HD:]], axis=-1).astype(jnp.bfloat16)
    keyval = lax.map(project, features)
    owners = image_slot[image_ids].astype(jnp.int32)

    def answer(inputs):
        request_queries, pair_slots = inputs
        joined = jnp.concatenate([keyval[pair_slots[0]], keyval[pair_slots[1]]], axis=0).astype(jnp.float32)
        scores = jnp.einsum('thgd,nhd->thgn', request_queries.astype(jnp.float32), joined[..., :HD], precision=highest)
        exponent = jnp.exp(scores).astype(jnp.bfloat16).astype(jnp.float32)
        denominator = lax.optimization_barrier(jnp.sum(exponent, axis=-1))
        numerator = jnp.einsum('thgn,nhd->thgd', exponent, joined[..., HD:], precision=highest)
        return numerator / denominator[..., None]
    result = lax.map(answer, (normed, owners))
    return (jnp.tanh(attn_gate[0]) * result).astype(jnp.bfloat16).reshape(ROWS, HEADS * HD)
```

```python
import functools

import jax
import jax.numpy as jnp
from jax import lax
from jax.experimental import pallas as pl
from jax.experimental.pallas import tpu as pltpu
from jax.sharding import PartitionSpec as P

epsilon = 1e-05
CAP = 4


def attend_kernel(q_ref, key_ref, value_ref, num_ref, den_ref):
    head = pl.program_id(0)
    scores = jnp.dot(q_ref[...], key_ref[...], preferred_element_type=jnp.float32)
    exponent = jnp.exp(scores).astype(jnp.bfloat16)
    width = num_ref.shape[1]
    both = jnp.dot(exponent, value_ref[...], preferred_element_type=jnp.float32)
    num_ref[...] = both[:, :width].astype(num_ref.dtype)
    total = both[:, width:]
    coarse = total.astype(jnp.bfloat16)
    fine = (total - coarse.astype(jnp.float32)).astype(jnp.bfloat16)
    lane = lax.broadcasted_iota(jnp.int32, total.shape, 1)
    heads = pl.num_programs(0)
    packed = jnp.where(
        lane == head,
        coarse.astype(jnp.float32),
        jnp.where(lane == head + heads, fine.astype(jnp.float32), 0.0),
    )

    @pl.when(head == 0)
    def _():
        den_ref[...] = jnp.zeros_like(den_ref)

    den_ref[...] += packed.astype(jnp.bfloat16)


def attend(queries, keys, values):
    rows, columns = queries.shape
    width, count = keys.shape
    heads = columns // width
    extended = jnp.concatenate([values, jnp.ones_like(values)], axis=1)
    return pl.pallas_call(
        attend_kernel,
        grid=(heads,),
        in_specs=[
            pl.BlockSpec((rows, width), lambda h: (0, h)),
            pl.BlockSpec((width, count), lambda h: (0, 0)),
            pl.BlockSpec((count, 2 * width), lambda h: (0, 0)),
        ],
        out_specs=[
            pl.BlockSpec((rows, width), lambda h: (0, h)),
            pl.BlockSpec((rows, width), lambda h: (0, 0)),
        ],
        out_shape=[
            jax.ShapeDtypeStruct((rows, columns), jnp.bfloat16),
            jax.ShapeDtypeStruct((rows, width), jnp.bfloat16),
        ],
        compiler_params=pltpu.CompilerParams(vmem_limit_bytes=40 << 20),
        name="attend",
    )(queries, keys, extended)


def slot_table(image_ids, image_slot, text_words):
    count = image_slot.shape[0]
    requests = image_ids.shape[0]
    matches = image_ids[:, :, None] == jnp.arange(count, dtype=jnp.int32)[None, None, :]
    owners = jnp.sum(jnp.where(matches, image_slot[None, None, :], 0), axis=-1)
    named = jnp.any(owners[:, :, None] == jnp.arange(count, dtype=jnp.int32), axis=1)
    earlier = jnp.arange(requests)[:, None] > jnp.arange(requests)[None, :]
    rank = jnp.sum(jnp.where(earlier[:, :, None], named[None].astype(jnp.int32), 0), axis=1)
    place = jnp.where(named, rank, CAP)
    picks = place.T[:, None, :] == jnp.arange(CAP, dtype=jnp.int32)[None, :, None]
    same = jnp.arange(text_words)[:, None] == jnp.arange(text_words)[None, :]
    table = picks[:, :, None, :, None] & same[None, None, :, None, :]
    return table.astype(jnp.bfloat16).reshape(
        count * CAP * text_words, requests * text_words
    )


def per_device(
    text_rows, q_weight, features, kv_weight, q_gain, k_gain, attn_gate, image_ids, image_slot
):
    rows = text_rows.shape[0]
    requests = image_ids.shape[0]
    words = rows // requests
    images = image_slot.shape[0]
    width = q_gain.shape[0]
    columns = q_weight.shape[1]
    group = columns // width
    heads_all = kv_weight.shape[1] // (2 * width)

    table = kv_weight.reshape(kv_weight.shape[0], heads_all, 2 * width)
    partial = jnp.einsum("nf,fhc->hcn", features[0], table, preferred_element_type=jnp.float32)
    parts = lax.all_to_all(partial.astype(jnp.bfloat16), "feat", 0, 0, tiled=True)
    summed = jnp.sum(parts.astype(jnp.float32), axis=0)
    key = summed[:width]
    key = key * lax.rsqrt(jnp.mean(key * key, axis=0, keepdims=True) + epsilon) * k_gain[:, None]
    key = key.astype(jnp.bfloat16)
    value = summed[width:].astype(jnp.bfloat16).T

    picks = slot_table(image_ids, image_slot, words)
    text = lax.all_gather(text_rows, "feat", axis=1, tiled=True)
    queries = jnp.dot(text, q_weight, preferred_element_type=jnp.float32)
    queries = queries.reshape(rows, group, width)
    queries = (
        queries
        * lax.rsqrt(jnp.mean(queries * queries, axis=-1, keepdims=True) + epsilon)
        * q_gain
        * width ** (-0.5)
    )
    queries = queries.astype(jnp.bfloat16).reshape(rows, columns)
    sent = jnp.dot(picks, queries, preferred_element_type=jnp.float32).astype(jnp.bfloat16)
    arrived = lax.all_to_all(
        sent.reshape(images, CAP * words, columns), "dp", 0, 0, tiled=True
    ).reshape(images * CAP * words, columns)

    numerator, denominator = attend(arrived, key, value)
    back = jnp.concatenate([numerator, denominator], axis=1)
    back = lax.all_to_all(
        back.reshape(images, CAP * words, columns + width), "dp", 0, 0, tiled=True
    ).reshape(images * CAP * words, columns + width)
    both = lax.dot_general(
        picks, back, (((0,), (0,)), ((), ())), preferred_element_type=jnp.float32
    )
    total = both[:, columns : columns + group] + both[:, columns + group : columns + 2 * group]
    result = both[:, :columns].reshape(rows, group, width) / total[:, :, None]
    return (jnp.tanh(attn_gate[0]) * result).astype(jnp.bfloat16).reshape(rows, columns)


def solution(mesh):
    in_specs = (
        P("dp", "feat"),
        P(None, "feat"),
        P("dp", None, "feat"),
        P("feat", None),
        P(),
        P(),
        P(),
        P("dp", None),
        P(),
    )
    return jax.shard_map(
        per_device, mesh=mesh, in_specs=in_specs, out_specs=P("dp", "feat"), check_vma=False
    )
```

```python
import functools

import jax
import jax.numpy as jnp
from jax import lax
from jax.experimental import pallas as pl
from jax.experimental.pallas import tpu as pltpu
from jax.sharding import PartitionSpec as P

epsilon = 1e-05
CAP = 4
RING = 4
KEY_SCALE = 64.0


def permute(values, across, along):
    pairs = [
        (side * RING + place, (side ^ across) * RING + (place + along) % RING)
        for side in range(2)
        for place in range(RING)
    ]
    return lax.ppermute(values, "feat", pairs)


def project_kernel(_, *refs):
    weights, (vision_ref, key_ref, value_ref) = refs[: 2 * RING], refs[2 * RING :]
    for part, out_ref in enumerate((key_ref, value_ref)):
        weight = jnp.concatenate([w[...] for w in weights[part::2]], axis=1)
        product = lax.dot_general(
            weight, vision_ref[...], (((0,), (0,)), ((), ())), preferred_element_type=jnp.float32
        )
        out_ref[...] = product.reshape(out_ref.shape).astype(out_ref.dtype)


def project(heads, kv_weight, vision, width, value_type):
    depth, tokens = vision.shape
    specs = [
        pl.BlockSpec((depth, width), functools.partial(lambda j, part, g, h: (0, 2 * h[j] + part), j, part))
        for j in range(RING)
        for part in range(2)
    ]
    out = pl.BlockSpec((RING, width, tokens), lambda g, h: (0, 0, 0))
    return pl.pallas_call(
        project_kernel,
        grid_spec=pltpu.PrefetchScalarGridSpec(
            num_scalar_prefetch=1,
            grid=(1,),
            in_specs=specs + [pl.BlockSpec((depth, tokens), lambda g, h: (0, 0))],
            out_specs=[out, out],
        ),
        out_shape=[
            jax.ShapeDtypeStruct((RING, width, tokens), jnp.float32),
            jax.ShapeDtypeStruct((RING, width, tokens), value_type),
        ],
        compiler_params=pltpu.CompilerParams(vmem_limit_bytes=24 << 20),
        name="project",
    )(heads, *([kv_weight] * (2 * RING)), vision)


def query_step_kernel(blocks, text_ref, weight_ref, *refs):
    total_ref, block_ref, sems = refs[-3:]
    count, _, depth = text_ref.shape
    copies = [
        pltpu.make_async_copy(
            weight_ref.at[pl.ds(pl.multiple_of(blocks[i] * depth, depth), depth)],
            block_ref.at[i],
            sems.at[i],
        )
        for i in range(count)
    ]
    for copy in copies:
        copy.start()
    total = refs[0][...] if len(refs) == 4 else None
    for i, copy in enumerate(copies):
        copy.wait()
        product = jnp.dot(text_ref[i], block_ref[i], preferred_element_type=jnp.float32)
        total = product if total is None else total + product
    total_ref[...] = total


def query_step(blocks, texts, weight, total=None):
    count, rows, depth = texts.shape
    columns = weight.shape[1]
    vmem = pl.BlockSpec(memory_space=pltpu.VMEM)
    return pl.pallas_call(
        query_step_kernel,
        grid_spec=pltpu.PrefetchScalarGridSpec(
            num_scalar_prefetch=1,
            grid=(),
            in_specs=[vmem, pl.BlockSpec(memory_space=pltpu.HBM)]
            + ([] if total is None else [vmem]),
            out_specs=vmem,
            scratch_shapes=[
                pltpu.VMEM((count, depth, columns), weight.dtype),
                pltpu.SemaphoreType.DMA((count,)),
            ],
        ),
        out_shape=jax.ShapeDtypeStruct((rows, columns), jnp.float32),
        compiler_params=pltpu.CompilerParams(vmem_limit_bytes=12 << 20),
        name="query_step",
    )(blocks, texts, weight, *(() if total is None else (total,)))


def place_requests(ids_ref, slots_ref, counts_ref, visit):
    images = slots_ref.shape[0]
    for image in range(images):
        counts_ref[image] = 0
    for request in range(ids_ref.shape[0]):
        for which in range(ids_ref.shape[1]):
            owner = slots_ref[ids_ref[request, which]]
            taken = counts_ref[owner]
            counts_ref[owner] = taken + 1
            visit(request, which, owner * CAP + taken)


def query_last_kernel(
    ids_ref, slots_ref, total_ref, gain_ref, out_ref, normed_ref, table_ref, counts_ref
):
    width = gain_ref.shape[1]
    heads = total_ref.shape[1] // width
    words = total_ref.shape[0] // ids_ref.shape[0]
    slots = out_ref.shape[0] // words
    for slot in range(slots):
        table_ref[slot] = 0

    def visit(request, _, slot):
        table_ref[slot] = request

    place_requests(ids_ref, slots_ref, counts_ref, visit)
    for head in range(heads):
        at = pl.ds(head * width, width)
        q = total_ref[:, at]
        q = q * lax.rsqrt(jnp.mean(q * q, axis=-1, keepdims=True) + epsilon) * gain_ref[...]
        normed_ref[:, at] = (q * width ** (-0.5)).astype(jnp.bfloat16).astype(jnp.float32)
    for slot in range(0, slots, 2):
        rows = [
            normed_ref[pl.ds(pl.multiple_of(table_ref[slot + i] * words, words), words)]
            for i in range(2)
        ]
        out_ref[pl.ds(slot * words, 2 * words)] = jnp.concatenate(rows).astype(jnp.bfloat16)


def query_last(image_ids, image_slot, total, gain):
    rows, columns = total.shape
    smem = pl.BlockSpec(memory_space=pltpu.SMEM)
    vmem = pl.BlockSpec(memory_space=pltpu.VMEM)
    images = image_slot.shape[0]
    words = rows // image_ids.shape[0]
    return pl.pallas_call(
        query_last_kernel,
        in_specs=[smem, smem, vmem, vmem],
        out_specs=vmem,
        out_shape=jax.ShapeDtypeStruct((images * CAP * words, columns), jnp.bfloat16),
        scratch_shapes=[
            pltpu.VMEM((rows, columns), jnp.float32),
            pltpu.SMEM((images * CAP,), jnp.int32),
            pltpu.SMEM((images,), jnp.int32),
        ],
        compiler_params=pltpu.CompilerParams(vmem_limit_bytes=8 << 20),
        name="query_last",
    )(image_ids, image_slot, total, gain[None])


def attend_kernel(q_ref, key_ref, value_ref, out_ref):
    width = key_ref.shape[0]
    heads = q_ref.shape[1] // width
    value = value_ref[...].T
    value = jnp.concatenate([value, jnp.ones_like(value)], axis=1)
    lane = lax.broadcasted_iota(jnp.int32, (q_ref.shape[0], width), 1)
    packed = jnp.zeros(lane.shape, jnp.float32)
    for head in range(heads):
        at = pl.ds(head * width, width)
        scores = jnp.dot(q_ref[:, at], key_ref[...], preferred_element_type=jnp.float32)
        exponent = jnp.exp(scores).astype(jnp.bfloat16)
        both = jnp.dot(exponent, value, preferred_element_type=jnp.float32)
        out_ref[:, at] = both[:, :width].astype(out_ref.dtype)
        total = both[:, width:]
        coarse = total.astype(jnp.bfloat16).astype(jnp.float32)
        packed = jnp.where(lane == head, coarse, packed)
        packed = jnp.where(lane == head + heads, total - coarse, packed)
    out_ref[:, pl.ds(heads * width, width)] = packed.astype(out_ref.dtype)


def attend(queries, keys, values):
    rows, columns = queries.shape
    vmem = pl.BlockSpec(memory_space=pltpu.VMEM)
    return pl.pallas_call(
        attend_kernel,
        in_specs=[vmem] * 3,
        out_specs=vmem,
        out_shape=jax.ShapeDtypeStruct((rows, columns + keys.shape[0]), jnp.bfloat16),
        compiler_params=pltpu.CompilerParams(vmem_limit_bytes=32 << 20),
        name="attend",
    )(queries, keys, values)


def combine_kernel(ids_ref, slots_ref, back_ref, gate_ref, out_ref, table_ref, counts_ref):
    requests, images = ids_ref.shape
    words = out_ref.shape[0] // requests
    columns = out_ref.shape[1]
    width = back_ref.shape[1] - columns
    heads = columns // width

    def visit(request, which, slot):
        table_ref[request * images + which] = slot

    place_requests(ids_ref, slots_ref, counts_ref, visit)
    gate = jnp.tanh(jnp.broadcast_to(gate_ref[...], (words, width)))
    for request in range(0, requests, 2):
        results = []
        for i in range(2):
            slots = [table_ref[(request + i) * images + which] for which in range(images)]
            parts = [
                back_ref[pl.ds(pl.multiple_of(slot * words, words), words)].astype(jnp.float32)
                for slot in slots
            ]
            both = parts[0] + parts[1]
            columns_of = []
            for head in range(heads):
                low = columns + head
                total = both[:, low : low + 1] + both[:, low + heads : low + heads + 1]
                at = slice(head * width, (head + 1) * width)
                columns_of.append(gate * (both[:, at] / total))
            results.append(jnp.concatenate(columns_of, axis=1))
        out_ref[pl.ds(request * words, 2 * words)] = jnp.concatenate(results).astype(out_ref.dtype)


def combine(image_ids, image_slot, back, gate, rows):
    smem = pl.BlockSpec(memory_space=pltpu.SMEM)
    vmem = pl.BlockSpec(memory_space=pltpu.VMEM)
    width = gate.shape[1]
    return pl.pallas_call(
        combine_kernel,
        in_specs=[smem, smem, vmem, vmem],
        out_specs=vmem,
        out_shape=jax.ShapeDtypeStruct((rows, back.shape[1] - width), jnp.bfloat16),
        scratch_shapes=[
            pltpu.SMEM((image_ids.size,), jnp.int32),
            pltpu.SMEM(image_slot.shape, jnp.int32),
        ],
        compiler_params=pltpu.CompilerParams(vmem_limit_bytes=8 << 20),
        name="combine",
    )(image_ids, image_slot, back, gate)


def per_device(
    text_rows, q_weight, features, kv_weight, q_gain, k_gain, attn_gate, image_ids, image_slot
):
    rows = text_rows.shape[0]
    words = rows // image_ids.shape[0]
    images = image_slot.shape[0]
    width = q_gain.shape[0]
    columns = q_weight.shape[1]

    mine = lax.axis_index("feat").astype(jnp.int32)
    side, place = mine >> 2, mine & (RING - 1)
    q_weight = pltpu.with_memory_space_constraint(q_weight, pltpu.HBM)
    near = (place + jnp.arange(RING, dtype=jnp.int32)) & (RING - 1)

    beside = permute(text_rows, 1, 0)

    vision = features[0].T
    key_away, value_away = project((1 - side) * RING + near, kv_weight, vision, width, jnp.bfloat16)
    key_away = (key_away * KEY_SCALE).astype(jnp.float16)
    key_away, beside = lax.optimization_barrier((key_away, beside))
    key_away = permute(key_away, 1, 0)
    both_texts = jnp.stack([text_rows, beside])
    passed = {step: permute(both_texts, 0, step) for step in (1, 3, 2)}
    key_home, value_home = project(side * RING + near, kv_weight, vision, width, jnp.float32)

    sides = jnp.stack([side, 1 - side]) * RING
    queries = query_step(sides + place, both_texts, q_weight)
    value_away, key_away, key_home, value_home, queries = lax.optimization_barrier(
        (value_away, key_away, key_home, value_home, queries)
    )
    value_away = permute(value_away, 1, 0)
    for step in (1, 3, 2):
        queries = query_step(sides + ((place - step) & (RING - 1)), passed[step], q_weight, queries)
    sent = query_last(image_ids, image_slot, queries, q_gain)
    sent, key_away = lax.optimization_barrier((sent, key_away))
    arrived = lax.all_to_all(
        sent.reshape(images, CAP * words, columns), "dp", 0, 0, tiled=True
    ).reshape(images * CAP * words, columns)

    def finish(home, away, wire, scale):
        def pair(step):
            return home[step] * scale + away[step].astype(jnp.float32)

        passed = [permute(pair(step).astype(wire), 0, step) for step in (1, 3, 2)]
        return functools.reduce(lambda t, p: t + p.astype(jnp.float32), passed, pair(0))

    key = finish(key_home, key_away, jnp.float16, KEY_SCALE)
    key = (
        key
        * lax.rsqrt(jnp.mean(key * key, axis=0, keepdims=True) + epsilon * KEY_SCALE**2)
        * k_gain[:, None]
    )
    key = key.astype(jnp.bfloat16)
    value = finish(value_home, value_away, jnp.bfloat16, 1.0).astype(jnp.bfloat16)

    back = attend(arrived, key, value)
    back = lax.all_to_all(
        back.reshape(images, CAP * words, columns + width), "dp", 0, 0, tiled=True
    ).reshape(images * CAP * words, columns + width)
    gate = jnp.broadcast_to(attn_gate[None], (1, width))
    return combine(image_ids, image_slot, back, gate, rows)


def solution(mesh):
    in_specs = (
        P("dp", "feat"),
        P(None, "feat"),
        P("dp", None, "feat"),
        P("feat", None),
        P(),
        P(),
        P(),
        P("dp", None),
        P(),
    )
    return jax.shard_map(
        per_device, mesh=mesh, in_specs=in_specs, out_specs=P("dp", "feat"), check_vma=False
    )
```

```python
import functools

import jax
import jax.numpy as jnp
from jax import lax
from jax.experimental import pallas as pl
from jax.experimental.pallas import tpu as pltpu
from jax.sharding import PartitionSpec as P

epsilon = 1e-05
CAP = 4
RING = 4
KEY_SCALE = 64.0
COST = pl.CostEstimate(flops=0, transcendentals=0, bytes_accessed=0)


def permute(values, across, along):
    pairs = [
        (side * RING + place, (side ^ across) * RING + (place + along) % RING)
        for side in range(2)
        for place in range(RING)
    ]
    return lax.ppermute(values, "feat", pairs)


def project_kernel(_, *refs, outs):
    vision_ref, out_refs = refs[-1 - outs], refs[-outs:]
    for out_ref in out_refs:
        count = out_ref.shape[0]
        weight = jnp.concatenate([w[...] for w in refs[:count]], axis=1)
        refs = refs[count:]
        product = lax.dot_general(
            weight, vision_ref[...], (((0,), (0,)), ((), ())), preferred_element_type=jnp.float32
        )
        out_ref[...] = product.reshape(out_ref.shape).astype(out_ref.dtype)


def device_at(mine, across, along):
    return ((mine[0] // RING) ^ across) * RING + ((mine[0] + along) & (RING - 1))


def project(mine, kv_weight, vision, width, outs, shape=jax.ShapeDtypeStruct):
    depth, tokens = vision.shape

    def block(across, part, along, _, mine):
        return 0, 2 * device_at(mine, across, along) + part

    return pl.pallas_call(
        functools.partial(project_kernel, outs=len(outs)),
        grid_spec=pltpu.PrefetchScalarGridSpec(
            num_scalar_prefetch=1,
            grid=(1,),
            in_specs=[
                pl.BlockSpec((depth, width), functools.partial(block, across, part, along))
                for across, part, _ in outs
                for along in range(RING)
            ]
            + [pl.BlockSpec((depth, tokens), lambda g, m: (0, 0))],
            out_specs=[pl.BlockSpec((RING, width, tokens), lambda g, m: (0, 0, 0))] * len(outs),
        ),
        out_shape=[shape((RING, width, tokens), kind) for _, _, kind in outs],
        compiler_params=pltpu.CompilerParams(vmem_limit_bytes=24 << 20),
        name="project",
        cost_estimate=COST,
    )(mine, *([kv_weight] * (RING * len(outs))), vision)


def add_products(mine, places, text_refs, weight_ref, block_ref, sems, total):
    pieces = [(ref, i) for ref in text_refs for i in range(ref.shape[0])]
    blocks = [device_at(mine, across, along) for across, along in places]
    depth = block_ref.shape[1]
    copies = [
        pltpu.make_async_copy(
            weight_ref.at[pl.ds(pl.multiple_of(blocks[n] * depth, depth), depth)],
            block_ref.at[n],
            sems.at[n],
        )
        for n in range(len(pieces))
    ]
    for copy in copies:
        copy.start()
    for n, (ref, i) in enumerate(pieces):
        copies[n].wait()
        product = jnp.dot(ref[i], block_ref[n], preferred_element_type=jnp.float32)
        total = product if total is None else total + product
    return total


def query_step_kernel(mine, *refs, places, first, count):
    texts, weight_ref = refs[:count], refs[count]
    total_ref, block_ref, sems = refs[-3:]
    total = None if first else refs[count + 1][...]
    total_ref[...] = add_products(mine, places, texts, weight_ref, block_ref, sems, total)


def step_scratch(texts, weight):
    pieces = sum(text.shape[0] for text in texts)
    return [
        pltpu.VMEM((pieces, texts[0].shape[2], weight.shape[1]), weight.dtype),
        pltpu.SemaphoreType.DMA((pieces,)),
    ]


def query_step(mine, places, texts, weight, total=None):
    vmem = pl.BlockSpec(memory_space=pltpu.VMEM)
    totals = () if total is None else (total,)
    return pl.pallas_call(
        functools.partial(
            query_step_kernel, places=places, first=total is None, count=len(texts)
        ),
        grid_spec=pltpu.PrefetchScalarGridSpec(
            num_scalar_prefetch=1,
            grid=(),
            in_specs=[vmem] * len(texts)
            + [pl.BlockSpec(memory_space=pltpu.HBM)]
            + [vmem] * len(totals),
            out_specs=vmem,
            scratch_shapes=step_scratch(texts, weight),
        ),
        out_shape=jax.ShapeDtypeStruct((texts[0].shape[1], weight.shape[1]), jnp.float32),
        compiler_params=pltpu.CompilerParams(vmem_limit_bytes=16 << 20),
        name="query_step",
        cost_estimate=COST,
    )(mine, *texts, weight, *totals)


def place_requests(ids_ref, slots_ref, counts_ref, visit):
    images = slots_ref.shape[0]
    for image in range(images):
        counts_ref[image] = 0
    for request in range(ids_ref.shape[0]):
        for which in range(ids_ref.shape[1]):
            owner = slots_ref[ids_ref[request, which]]
            taken = counts_ref[owner]
            counts_ref[owner] = taken + 1
            visit(request, which, owner * CAP + taken)


def query_last_kernel(mine, ids_ref, slots_ref, *refs, places, count):
    texts, (weight_ref, total_ref, gain_ref, out_ref) = refs[:count], refs[count : count + 4]
    normed_ref, table_ref, counts_ref, block_ref, sems = refs[count + 4 :]
    width = gain_ref.shape[1]
    heads = total_ref.shape[1] // width
    words = total_ref.shape[0] // ids_ref.shape[0]
    slots = out_ref.shape[0] // words
    total = add_products(mine, places, texts, weight_ref, block_ref, sems, total_ref[...])
    for slot in range(slots):
        table_ref[slot] = 0

    def visit(request, _, slot):
        table_ref[slot] = request

    place_requests(ids_ref, slots_ref, counts_ref, visit)
    for head in range(heads):
        at = slice(head * width, (head + 1) * width)
        q = total[:, at]
        q = q * lax.rsqrt(jnp.mean(q * q, axis=-1, keepdims=True) + epsilon) * gain_ref[...]
        normed_ref[:, at] = (q * width ** (-0.5)).astype(jnp.bfloat16).astype(jnp.float32)
    for slot in range(0, slots, 2):
        rows = [
            normed_ref[pl.ds(pl.multiple_of(table_ref[slot + i] * words, words), words)]
            for i in range(2)
        ]
        out_ref[pl.ds(slot * words, 2 * words)] = jnp.concatenate(rows).astype(jnp.bfloat16)


def query_last(mine, places, image_ids, image_slot, texts, weight, total, gain):
    rows, columns = total.shape
    smem = pl.BlockSpec(memory_space=pltpu.SMEM)
    vmem = pl.BlockSpec(memory_space=pltpu.VMEM)
    images = image_slot.shape[0]
    words = rows // image_ids.shape[0]
    return pl.pallas_call(
        functools.partial(query_last_kernel, places=places, count=len(texts)),
        grid_spec=pltpu.PrefetchScalarGridSpec(
            num_scalar_prefetch=1,
            grid=(),
            in_specs=[smem, smem]
            + [vmem] * len(texts)
            + [pl.BlockSpec(memory_space=pltpu.HBM), vmem, vmem],
            out_specs=vmem,
            scratch_shapes=[
                pltpu.VMEM((rows, columns), jnp.float32),
                pltpu.SMEM((images * CAP,), jnp.int32),
                pltpu.SMEM((images,), jnp.int32),
            ]
            + step_scratch(texts, weight),
        ),
        out_shape=jax.ShapeDtypeStruct((images * CAP * words, columns), jnp.bfloat16),
        compiler_params=pltpu.CompilerParams(vmem_limit_bytes=16 << 20),
        name="query_last",
    )(mine, image_ids, image_slot, *texts, weight, total, gain[None])


def attend_kernel(q_ref, key_ref, value_ref, out_ref):
    width = key_ref.shape[0]
    heads = q_ref.shape[1] // width
    value = value_ref[...].T
    value = jnp.concatenate([value, jnp.ones_like(value)], axis=1)
    lane = lax.broadcasted_iota(jnp.int32, (q_ref.shape[0], width), 1)
    packed = jnp.zeros(lane.shape, jnp.float32)
    for head in range(heads):
        at = pl.ds(head * width, width)
        scores = jnp.dot(q_ref[:, at], key_ref[...], preferred_element_type=jnp.float32)
        exponent = jnp.exp(scores).astype(jnp.bfloat16)
        both = jnp.dot(exponent, value, preferred_element_type=jnp.float32)
        out_ref[:, at] = both[:, :width].astype(out_ref.dtype)
        total = both[:, width:]
        coarse = total.astype(jnp.bfloat16).astype(jnp.float32)
        packed = jnp.where(lane == head, coarse, packed)
        packed = jnp.where(lane == head + heads, total - coarse, packed)
    out_ref[:, pl.ds(heads * width, width)] = packed.astype(out_ref.dtype)


def attend(queries, keys, values):
    rows, columns = queries.shape
    vmem = pl.BlockSpec(memory_space=pltpu.VMEM)
    return pl.pallas_call(
        attend_kernel,
        in_specs=[vmem] * 3,
        out_specs=vmem,
        out_shape=jax.ShapeDtypeStruct((rows, columns + keys.shape[0]), jnp.bfloat16),
        compiler_params=pltpu.CompilerParams(vmem_limit_bytes=32 << 20),
        name="attend",
    )(queries, keys, values)


def combine_kernel(ids_ref, slots_ref, back_ref, gate_ref, out_ref, table_ref, counts_ref):
    requests, images = ids_ref.shape
    words = out_ref.shape[0] // requests
    columns = out_ref.shape[1]
    width = back_ref.shape[1] - columns
    heads = columns // width

    def visit(request, which, slot):
        table_ref[request * images + which] = slot

    place_requests(ids_ref, slots_ref, counts_ref, visit)
    gate = jnp.tanh(jnp.broadcast_to(gate_ref[...], (words, width)))
    for request in range(0, requests, 2):
        results = []
        for i in range(2):
            slots = [table_ref[(request + i) * images + which] for which in range(images)]
            parts = [
                back_ref[pl.ds(pl.multiple_of(slot * words, words), words)].astype(jnp.float32)
                for slot in slots
            ]
            both = parts[0] + parts[1]
            columns_of = []
            for head in range(heads):
                low = columns + head
                total = both[:, low : low + 1] + both[:, low + heads : low + heads + 1]
                at = slice(head * width, (head + 1) * width)
                columns_of.append(gate * (both[:, at] / total))
            results.append(jnp.concatenate(columns_of, axis=1))
        out_ref[pl.ds(request * words, 2 * words)] = jnp.concatenate(results).astype(out_ref.dtype)


def combine(image_ids, image_slot, back, gate, rows):
    smem = pl.BlockSpec(memory_space=pltpu.SMEM)
    vmem = pl.BlockSpec(memory_space=pltpu.VMEM)
    width = gate.shape[1]
    return pl.pallas_call(
        combine_kernel,
        in_specs=[smem, smem, vmem, vmem],
        out_specs=vmem,
        out_shape=jax.ShapeDtypeStruct((rows, back.shape[1] - width), jnp.bfloat16),
        scratch_shapes=[
            pltpu.SMEM((image_ids.size,), jnp.int32),
            pltpu.SMEM(image_slot.shape, jnp.int32),
        ],
        compiler_params=pltpu.CompilerParams(vmem_limit_bytes=8 << 20),
        name="combine",
    )(image_ids, image_slot, back, gate)


def per_device(
    text_rows, q_weight, features, kv_weight, q_gain, k_gain, attn_gate, image_ids, image_slot
):
    rows = text_rows.shape[0]
    words = rows // image_ids.shape[0]
    images = image_slot.shape[0]
    width = q_gain.shape[0]
    columns = q_weight.shape[1]

    mine = lax.axis_index("feat").astype(jnp.int32).reshape(1)
    kv_weight = pltpu.with_memory_space_constraint(kv_weight, pltpu.HBM)
    q_weight = pltpu.with_memory_space_constraint(q_weight, pltpu.HBM)

    beside = permute(text_rows, 1, 0)

    vision = features[0].T
    (key_away,) = project(mine, kv_weight, vision, width, [(1, 0, jnp.float32)])
    key_away = (key_away * KEY_SCALE).astype(jnp.float16)
    key_away, beside = lax.optimization_barrier((key_away, beside))
    key_away = permute(key_away, 1, 0)

    both_texts = jnp.stack([text_rows, beside])
    before = permute(both_texts, 0, 1)
    behind = permute(both_texts, 0, RING - 1)

    queries = query_step(mine, [(0, 0), (1, 0)], [both_texts], q_weight)
    mine, queries = lax.optimization_barrier((mine, queries))
    value_away, key_home, value_home = project(
        mine,
        kv_weight,
        vision,
        width,
        [(1, 1, jnp.bfloat16), (0, 0, jnp.float32), (0, 1, jnp.float32)],
        pltpu.HBM,
    )
    before, behind, value_away = lax.optimization_barrier((before, behind, value_away))
    around = [permute(before[:1], 0, 1), permute(behind[1:], 0, RING - 1)]
    value_away = permute(value_away, 1, 0)
    places = [(0, -1), (1, -1), (0, 1), (1, 1)]
    queries = query_step(mine, places, [before, behind], q_weight, queries)
    key_away, queries = lax.optimization_barrier((key_away, queries))
    sent = query_last(
        mine, [(0, 2), (1, 2)], image_ids, image_slot, around, q_weight, queries, q_gain
    )
    sent, key_away = lax.optimization_barrier((sent, key_away))
    arrived = lax.all_to_all(
        sent.reshape(images, CAP * words, columns), "dp", 0, 0, tiled=True
    ).reshape(images * CAP * words, columns)

    def finish(home, away, wire, scale):
        def pair(step):
            return home[step] * scale + away[step].astype(jnp.float32)

        passed = [permute(pair(step).astype(wire), 0, step) for step in (1, 3, 2)]
        return functools.reduce(lambda t, p: t + p.astype(jnp.float32), passed, pair(0))

    key = finish(key_home, key_away, jnp.float16, KEY_SCALE)
    key = (
        key
        * lax.rsqrt(jnp.mean(key * key, axis=0, keepdims=True) + epsilon * KEY_SCALE**2)
        * k_gain[:, None]
    )
    key = key.astype(jnp.bfloat16)
    value = finish(value_home, value_away, jnp.bfloat16, 1.0).astype(jnp.bfloat16)

    back = attend(arrived, key, value)
    back = lax.all_to_all(
        back.reshape(images, CAP * words, columns + width), "dp", 0, 0, tiled=True
    ).reshape(images * CAP * words, columns + width)
    gate = jnp.broadcast_to(attn_gate[None], (1, width))
    return combine(image_ids, image_slot, back, gate, rows)


def solution(mesh):
    in_specs = (
        P("dp", "feat"),
        P(None, "feat"),
        P("dp", None, "feat"),
        P("feat", None),
        P(),
        P(),
        P(),
        P("dp", None),
        P(),
    )
    return jax.shard_map(
        per_device, mesh=mesh, in_specs=in_specs, out_specs=P("dp", "feat"), check_vma=False
    )
```

```python
import functools

import jax
import jax.numpy as jnp
from jax import lax
from jax.experimental import pallas as pl
from jax.experimental.pallas import tpu as pltpu
from jax.sharding import PartitionSpec as P

epsilon = 1e-05
CAP = 4
RING = 4
KEY_SCALE = 64.0
COST = pl.CostEstimate(flops=0, transcendentals=0, bytes_accessed=0)


def permute(values, across, along):
    pairs = [
        (side * RING + place, (side ^ across) * RING + (place + along) % RING)
        for side in range(2)
        for place in range(RING)
    ]
    return lax.ppermute(values, "feat", pairs)


def project_kernel(_, *refs, outs):
    vision_ref, out_refs = refs[-1 - outs], refs[-outs:]
    for out_ref in out_refs:
        count = out_ref.shape[0]
        weight = jnp.concatenate([w[...] for w in refs[:count]], axis=1)
        refs = refs[count:]
        product = lax.dot_general(
            weight, vision_ref[...], (((0,), (0,)), ((), ())), preferred_element_type=jnp.float32
        )
        out_ref[...] = product.reshape(out_ref.shape).astype(out_ref.dtype)


def device_at(mine, across, along):
    return ((mine[0] // RING) ^ across) * RING + ((mine[0] + along) & (RING - 1))


def project(mine, kv_weight, vision, width, outs, shape=jax.ShapeDtypeStruct):
    depth, tokens = vision.shape

    def block(across, part, along, _, mine):
        return 0, 2 * device_at(mine, across, along) + part

    return pl.pallas_call(
        functools.partial(project_kernel, outs=len(outs)),
        grid_spec=pltpu.PrefetchScalarGridSpec(
            num_scalar_prefetch=1,
            grid=(1,),
            in_specs=[
                pl.BlockSpec((depth, width), functools.partial(block, across, part, along))
                for across, part, _ in outs
                for along in range(RING)
            ]
            + [pl.BlockSpec((depth, tokens), lambda g, m: (0, 0))],
            out_specs=[pl.BlockSpec((RING, width, tokens), lambda g, m: (0, 0, 0))] * len(outs),
        ),
        out_shape=[shape((RING, width, tokens), kind) for _, _, kind in outs],
        compiler_params=pltpu.CompilerParams(vmem_limit_bytes=24 << 20),
        name="project",
        cost_estimate=COST,
    )(mine, *([kv_weight] * (RING * len(outs))), vision)


def add_products(mine, places, text_refs, weight_ref, block_ref, sems, total):
    pieces = [(ref, i) for ref in text_refs for i in range(ref.shape[0])]
    blocks = [device_at(mine, across, along) for across, along in places]
    depth = block_ref.shape[1]
    copies = [
        pltpu.make_async_copy(
            weight_ref.at[pl.ds(pl.multiple_of(blocks[n] * depth, depth), depth)],
            block_ref.at[n],
            sems.at[n],
        )
        for n in range(len(pieces))
    ]
    for copy in copies:
        copy.start()
    for n, (ref, i) in enumerate(pieces):
        copies[n].wait()
        product = jnp.dot(ref[i], block_ref[n], preferred_element_type=jnp.float32)
        total = product if total is None else total + product
    return total


def query_step_kernel(mine, *refs, places, first, count):
    texts, weight_ref = refs[:count], refs[count]
    total_ref, block_ref, sems = refs[-3:]
    total = None if first else refs[count + 1][...]
    total_ref[...] = add_products(mine, places, texts, weight_ref, block_ref, sems, total)


def step_scratch(texts, weight):
    pieces = sum(text.shape[0] for text in texts)
    return [
        pltpu.VMEM((pieces, texts[0].shape[2], weight.shape[1]), weight.dtype),
        pltpu.SemaphoreType.DMA((pieces,)),
    ]


def query_step(mine, places, texts, weight, total=None):
    vmem = pl.BlockSpec(memory_space=pltpu.VMEM)
    totals = () if total is None else (total,)
    return pl.pallas_call(
        functools.partial(
            query_step_kernel, places=places, first=total is None, count=len(texts)
        ),
        grid_spec=pltpu.PrefetchScalarGridSpec(
            num_scalar_prefetch=1,
            grid=(),
            in_specs=[vmem] * len(texts)
            + [pl.BlockSpec(memory_space=pltpu.HBM)]
            + [vmem] * len(totals),
            out_specs=vmem,
            scratch_shapes=step_scratch(texts, weight),
        ),
        out_shape=jax.ShapeDtypeStruct((texts[0].shape[1], weight.shape[1]), jnp.float32),
        compiler_params=pltpu.CompilerParams(vmem_limit_bytes=16 << 20),
        name="query_step",
        cost_estimate=COST,
    )(mine, *texts, weight, *totals)


def place_requests(ids_ref, slots_ref, counts_ref, visit):
    images = slots_ref.shape[0]
    for image in range(images):
        counts_ref[image] = 0
    for request in range(ids_ref.shape[0]):
        for which in range(ids_ref.shape[1]):
            owner = slots_ref[ids_ref[request, which]]
            taken = counts_ref[owner]
            counts_ref[owner] = taken + 1
            visit(request, which, owner * CAP + taken)


def query_last_kernel(mine, ids_ref, slots_ref, *refs, places, count):
    texts, (weight_ref, total_ref, gain_ref, out_ref) = refs[:count], refs[count : count + 4]
    normed_ref, table_ref, counts_ref, block_ref, sems = refs[count + 4 :]
    width = gain_ref.shape[1]
    heads = total_ref.shape[1] // width
    words = total_ref.shape[0] // ids_ref.shape[0]
    slots = out_ref.shape[0] // words
    total = add_products(mine, places, texts, weight_ref, block_ref, sems, total_ref[...])
    for slot in range(slots):
        table_ref[slot] = 0

    def visit(request, _, slot):
        table_ref[slot] = request

    place_requests(ids_ref, slots_ref, counts_ref, visit)
    for head in range(heads):
        at = slice(head * width, (head + 1) * width)
        q = total[:, at]
        q = q * lax.rsqrt(jnp.mean(q * q, axis=-1, keepdims=True) + epsilon) * gain_ref[...]
        normed_ref[:, at] = (q * width ** (-0.5)).astype(jnp.bfloat16).astype(jnp.float32)
    for slot in range(0, slots, 2):
        rows = [
            normed_ref[pl.ds(pl.multiple_of(table_ref[slot + i] * words, words), words)]
            for i in range(2)
        ]
        out_ref[pl.ds(slot * words, 2 * words)] = jnp.concatenate(rows).astype(jnp.bfloat16)


def query_last(mine, places, image_ids, image_slot, texts, weight, total, gain):
    rows, columns = total.shape
    smem = pl.BlockSpec(memory_space=pltpu.SMEM)
    vmem = pl.BlockSpec(memory_space=pltpu.VMEM)
    images = image_slot.shape[0]
    words = rows // image_ids.shape[0]
    return pl.pallas_call(
        functools.partial(query_last_kernel, places=places, count=len(texts)),
        grid_spec=pltpu.PrefetchScalarGridSpec(
            num_scalar_prefetch=1,
            grid=(),
            in_specs=[smem, smem]
            + [vmem] * len(texts)
            + [pl.BlockSpec(memory_space=pltpu.HBM), vmem, vmem],
            out_specs=vmem,
            scratch_shapes=[
                pltpu.VMEM((rows, columns), jnp.float32),
                pltpu.SMEM((images * CAP,), jnp.int32),
                pltpu.SMEM((images,), jnp.int32),
            ]
            + step_scratch(texts, weight),
        ),
        out_shape=jax.ShapeDtypeStruct((images * CAP * words, columns), jnp.bfloat16),
        compiler_params=pltpu.CompilerParams(vmem_limit_bytes=16 << 20),
        name="query_last",
    )(mine, image_ids, image_slot, *texts, weight, total, gain[None])


def attend_kernel(q_ref, key_ref, value_ref, out_ref):
    width = key_ref.shape[0]
    heads = q_ref.shape[1] // width
    value = value_ref[...].T
    value = jnp.concatenate([value, jnp.ones_like(value)], axis=1)
    lane = lax.broadcasted_iota(jnp.int32, (q_ref.shape[0], width), 1)
    packed = jnp.zeros(lane.shape, jnp.float32)
    for head in range(heads):
        at = pl.ds(head * width, width)
        scores = jnp.dot(q_ref[:, at], key_ref[...], preferred_element_type=jnp.float32)
        exponent = jnp.exp(scores).astype(jnp.bfloat16)
        both = jnp.dot(exponent, value, preferred_element_type=jnp.float32)
        out_ref[:, at] = both[:, :width].astype(out_ref.dtype)
        total = both[:, width:]
        coarse = total.astype(jnp.bfloat16).astype(jnp.float32)
        packed = jnp.where(lane == head, coarse, packed)
        packed = jnp.where(lane == head + heads, total - coarse, packed)
    out_ref[:, pl.ds(heads * width, width)] = packed.astype(out_ref.dtype)


def attend(queries, keys, values):
    rows, columns = queries.shape
    vmem = pl.BlockSpec(memory_space=pltpu.VMEM)
    return pl.pallas_call(
        attend_kernel,
        in_specs=[vmem] * 3,
        out_specs=vmem,
        out_shape=jax.ShapeDtypeStruct((rows, columns + keys.shape[0]), jnp.bfloat16),
        compiler_params=pltpu.CompilerParams(vmem_limit_bytes=32 << 20),
        name="attend",
    )(queries, keys, values)


def combine_kernel(ids_ref, slots_ref, back_ref, gate_ref, out_ref, table_ref, counts_ref):
    requests, images = ids_ref.shape
    words = out_ref.shape[0] // requests
    columns = out_ref.shape[1]
    width = back_ref.shape[1] - columns
    heads = columns // width

    def visit(request, which, slot):
        table_ref[request * images + which] = slot

    place_requests(ids_ref, slots_ref, counts_ref, visit)
    gate = jnp.tanh(jnp.broadcast_to(gate_ref[...], (words, width)))
    for request in range(0, requests, 2):
        results = []
        for i in range(2):
            slots = [table_ref[(request + i) * images + which] for which in range(images)]
            parts = [
                back_ref[pl.ds(pl.multiple_of(slot * words, words), words)].astype(jnp.float32)
                for slot in slots
            ]
            both = parts[0] + parts[1]
            columns_of = []
            for head in range(heads):
                low = columns + head
                total = both[:, low : low + 1] + both[:, low + heads : low + heads + 1]
                at = slice(head * width, (head + 1) * width)
                columns_of.append(gate * (both[:, at] / total))
            results.append(jnp.concatenate(columns_of, axis=1))
        out_ref[pl.ds(request * words, 2 * words)] = jnp.concatenate(results).astype(out_ref.dtype)


def combine(image_ids, image_slot, back, gate, rows):
    smem = pl.BlockSpec(memory_space=pltpu.SMEM)
    vmem = pl.BlockSpec(memory_space=pltpu.VMEM)
    width = gate.shape[1]
    return pl.pallas_call(
        combine_kernel,
        in_specs=[smem, smem, vmem, vmem],
        out_specs=vmem,
        out_shape=jax.ShapeDtypeStruct((rows, back.shape[1] - width), jnp.bfloat16),
        scratch_shapes=[
            pltpu.SMEM((image_ids.size,), jnp.int32),
            pltpu.SMEM(image_slot.shape, jnp.int32),
        ],
        compiler_params=pltpu.CompilerParams(vmem_limit_bytes=8 << 20),
        name="combine",
    )(image_ids, image_slot, back, gate)


def per_device(
    text_rows, q_weight, features, kv_weight, q_gain, k_gain, attn_gate, image_ids, image_slot
):
    rows = text_rows.shape[0]
    words = rows // image_ids.shape[0]
    images = image_slot.shape[0]
    width = q_gain.shape[0]
    columns = q_weight.shape[1]

    mine = lax.axis_index("feat").astype(jnp.int32).reshape(1)
    kv_weight = pltpu.with_memory_space_constraint(kv_weight, pltpu.HBM)
    q_weight = pltpu.with_memory_space_constraint(q_weight, pltpu.HBM)

    beside = permute(text_rows, 1, 0)

    vision = pltpu.with_memory_space_constraint(features[0].T, pltpu.HBM)
    (key_away,) = project(mine, kv_weight, vision, width, [(1, 0, jnp.float32)])
    key_away = (key_away * KEY_SCALE).astype(jnp.float16)
    key_away = permute(key_away, 1, 0)

    both_texts = jnp.stack([text_rows, beside])
    before = permute(both_texts, 0, 1)
    behind = permute(both_texts, 0, RING - 1)

    queries = query_step(mine, [(0, 0), (1, 0)], [both_texts], q_weight)
    mine, queries = lax.optimization_barrier((mine, queries))
    value_away, key_home, value_home = project(
        mine,
        kv_weight,
        vision,
        width,
        [(1, 1, jnp.bfloat16), (0, 0, jnp.float32), (0, 1, jnp.float32)],
        pltpu.HBM,
    )
    before, value_away = lax.optimization_barrier((before, value_away))
    around = [permute(before[:1], 0, 1), permute(behind[1:], 0, RING - 1)]
    value_away = permute(value_away, 1, 0)
    places = [(0, -1), (1, -1), (0, 1), (1, 1)]
    queries = query_step(mine, places, [before, behind], q_weight, queries)
    key_away, queries = lax.optimization_barrier((key_away, queries))
    sent = query_last(
        mine, [(0, 2), (1, 2)], image_ids, image_slot, around, q_weight, queries, q_gain
    )
    sent, key_away = lax.optimization_barrier((sent, key_away))
    arrived = lax.all_to_all(
        sent.reshape(images, CAP * words, columns), "dp", 0, 0, tiled=True
    ).reshape(images * CAP * words, columns)

    def finish(home, away, wire, scale):
        def pair(step):
            return home[step] * scale + away[step].astype(jnp.float32)

        passed = [permute(pair(step).astype(wire), 0, step) for step in (1, 3, 2)]
        return functools.reduce(lambda t, p: t + p.astype(jnp.float32), passed, pair(0))

    key = finish(key_home, key_away, jnp.float16, KEY_SCALE)
    key = (
        key
        * lax.rsqrt(jnp.mean(key * key, axis=0, keepdims=True) + epsilon * KEY_SCALE**2)
        * k_gain[:, None]
    )
    key = key.astype(jnp.bfloat16)
    value = finish(value_home, value_away, jnp.bfloat16, 1.0).astype(jnp.bfloat16)

    back = attend(arrived, key, value)
    back = lax.all_to_all(
        back.reshape(images, CAP * words, columns + width), "dp", 0, 0, tiled=True
    ).reshape(images * CAP * words, columns + width)
    gate = jnp.broadcast_to(attn_gate[None], (1, width))
    return combine(image_ids, image_slot, back, gate, rows)


def solution(mesh):
    in_specs = (
        P("dp", "feat"),
        P(None, "feat"),
        P("dp", None, "feat"),
        P("feat", None),
        P(),
        P(),
        P(),
        P("dp", None),
        P(),
    )
    return jax.shard_map(
        per_device, mesh=mesh, in_specs=in_specs, out_specs=P("dp", "feat"), check_vma=False
    )
```

```python
import functools

import jax
import jax.numpy as jnp
from jax import lax
from jax.experimental import pallas as pl
from jax.experimental.pallas import tpu as pltpu
from jax.sharding import PartitionSpec as P

epsilon = 1e-05
CAP = 4
RING = 4
KEY_SCALE = 64.0
COST = pl.CostEstimate(flops=0, transcendentals=0, bytes_accessed=0)


def permute(values, across, along):
    pairs = [
        (side * RING + place, (side ^ across) * RING + (place + along) % RING)
        for side in range(2)
        for place in range(RING)
    ]
    return lax.ppermute(values, "feat", pairs)


def project_kernel(_, *refs, outs):
    vision_ref, out_refs = refs[-1 - outs], refs[-outs:]
    for out_ref in out_refs:
        count = out_ref.shape[0]
        weight = jnp.concatenate([w[...] for w in refs[:count]], axis=1)
        refs = refs[count:]
        product = lax.dot_general(
            weight, vision_ref[...], (((0,), (0,)), ((), ())), preferred_element_type=jnp.float32
        )
        out_ref[...] = product.reshape(out_ref.shape).astype(out_ref.dtype)


def device_at(mine, across, along):
    return ((mine[0] // RING) ^ across) * RING + ((mine[0] + along) & (RING - 1))


def project(mine, kv_weight, vision, width, outs, parts, shape=jax.ShapeDtypeStruct):
    depth, tokens = vision.shape

    def block(across, part, along, _, mine):
        return 0, 2 * device_at(mine, across, along) + part

    return pl.pallas_call(
        functools.partial(project_kernel, outs=len(outs)),
        grid_spec=pltpu.PrefetchScalarGridSpec(
            num_scalar_prefetch=1,
            grid=(parts,),
            in_specs=[
                pl.BlockSpec((depth, width), functools.partial(block, across, part, along))
                for across, part, _ in outs
                for along in range(RING)
            ]
            + [pl.BlockSpec((depth, tokens // parts), lambda g, m: (0, g))],
            out_specs=[pl.BlockSpec((RING, width, tokens // parts), lambda g, m: (0, 0, g))] * len(outs),
        ),
        out_shape=[shape((RING, width, tokens), kind) for _, _, kind in outs],
        compiler_params=pltpu.CompilerParams(vmem_limit_bytes=24 << 20),
        name="project",
        cost_estimate=COST,
    )(mine, *([kv_weight] * (RING * len(outs))), vision)


def add_products(mine, places, text_refs, weight_ref, block_ref, sems, total):
    pieces = [(ref, i) for ref in text_refs for i in range(ref.shape[0])]
    blocks = [device_at(mine, across, along) for across, along in places]
    depth = block_ref.shape[1]
    copies = [
        pltpu.make_async_copy(
            weight_ref.at[pl.ds(pl.multiple_of(blocks[n] * depth, depth), depth)],
            block_ref.at[n],
            sems.at[n],
        )
        for n in range(len(pieces))
    ]
    for copy in copies:
        copy.start()
    for n, (ref, i) in enumerate(pieces):
        copies[n].wait()
        product = jnp.dot(ref[i], block_ref[n], preferred_element_type=jnp.float32)
        total = product if total is None else total + product
    return total


def query_step_kernel(mine, *refs, places, first, count):
    texts, weight_ref = refs[:count], refs[count]
    total_ref, block_ref, sems = refs[-3:]
    total = None if first else refs[count + 1][...]
    total_ref[...] = add_products(mine, places, texts, weight_ref, block_ref, sems, total)


def step_scratch(texts, weight):
    pieces = sum(text.shape[0] for text in texts)
    return [
        pltpu.VMEM((pieces, texts[0].shape[2], weight.shape[1]), weight.dtype),
        pltpu.SemaphoreType.DMA((pieces,)),
    ]


def query_step(mine, places, texts, weight, total=None):
    vmem = pl.BlockSpec(memory_space=pltpu.VMEM)
    totals = () if total is None else (total,)
    return pl.pallas_call(
        functools.partial(
            query_step_kernel, places=places, first=total is None, count=len(texts)
        ),
        grid_spec=pltpu.PrefetchScalarGridSpec(
            num_scalar_prefetch=1,
            grid=(),
            in_specs=[vmem] * len(texts)
            + [pl.BlockSpec(memory_space=pltpu.HBM)]
            + [vmem] * len(totals),
            out_specs=vmem,
            scratch_shapes=step_scratch(texts, weight),
        ),
        out_shape=jax.ShapeDtypeStruct((texts[0].shape[1], weight.shape[1]), jnp.float32),
        compiler_params=pltpu.CompilerParams(vmem_limit_bytes=16 << 20),
        name="query_step",
        cost_estimate=COST,
    )(mine, *texts, weight, *totals)


def place_requests(ids_ref, slots_ref, counts_ref, visit):
    images = slots_ref.shape[0]
    for image in range(images):
        counts_ref[image] = 0
    for request in range(ids_ref.shape[0]):
        for which in range(ids_ref.shape[1]):
            owner = slots_ref[ids_ref[request, which]]
            taken = counts_ref[owner]
            counts_ref[owner] = taken + 1
            visit(request, which, owner * CAP + taken)


def query_last_kernel(mine, ids_ref, slots_ref, *refs, places, count):
    texts, (weight_ref, total_ref, gain_ref, out_ref) = refs[:count], refs[count : count + 4]
    normed_ref, table_ref, counts_ref, block_ref, sems = refs[count + 4 :]
    width = gain_ref.shape[1]
    heads = total_ref.shape[1] // width
    words = total_ref.shape[0] // ids_ref.shape[0]
    slots = out_ref.shape[0] // words
    total = add_products(mine, places, texts, weight_ref, block_ref, sems, total_ref[...])
    for slot in range(slots):
        table_ref[slot] = 0

    def visit(request, _, slot):
        table_ref[slot] = request

    place_requests(ids_ref, slots_ref, counts_ref, visit)
    for head in range(heads):
        at = slice(head * width, (head + 1) * width)
        q = total[:, at]
        q = q * lax.rsqrt(jnp.mean(q * q, axis=-1, keepdims=True) + epsilon) * gain_ref[...]
        normed_ref[:, at] = (q * width ** (-0.5)).astype(jnp.bfloat16).astype(jnp.float32)
    for slot in range(0, slots, 2):
        rows = [
            normed_ref[pl.ds(pl.multiple_of(table_ref[slot + i] * words, words), words)]
            for i in range(2)
        ]
        out_ref[pl.ds(slot * words, 2 * words)] = jnp.concatenate(rows).astype(jnp.bfloat16)


def query_last(mine, places, image_ids, image_slot, texts, weight, total, gain):
    rows, columns = total.shape
    smem = pl.BlockSpec(memory_space=pltpu.SMEM)
    vmem = pl.BlockSpec(memory_space=pltpu.VMEM)
    images = image_slot.shape[0]
    words = rows // image_ids.shape[0]
    return pl.pallas_call(
        functools.partial(query_last_kernel, places=places, count=len(texts)),
        grid_spec=pltpu.PrefetchScalarGridSpec(
            num_scalar_prefetch=1,
            grid=(),
            in_specs=[smem, smem]
            + [vmem] * len(texts)
            + [pl.BlockSpec(memory_space=pltpu.HBM), vmem, vmem],
            out_specs=vmem,
            scratch_shapes=[
                pltpu.VMEM((rows, columns), jnp.float32),
                pltpu.SMEM((images * CAP,), jnp.int32),
                pltpu.SMEM((images,), jnp.int32),
            ]
            + step_scratch(texts, weight),
        ),
        out_shape=jax.ShapeDtypeStruct((images * CAP * words, columns), jnp.bfloat16),
        compiler_params=pltpu.CompilerParams(vmem_limit_bytes=16 << 20),
        name="query_last",
    )(mine, image_ids, image_slot, *texts, weight, total, gain[None])


def attend_kernel(q_ref, key_ref, value_ref, out_ref):
    width = key_ref.shape[0]
    heads = q_ref.shape[1] // width
    value = value_ref[...].T
    value = jnp.concatenate([value, jnp.ones_like(value)], axis=1)
    lane = lax.broadcasted_iota(jnp.int32, (q_ref.shape[0], width), 1)
    packed = jnp.zeros(lane.shape, jnp.float32)
    for head in range(heads):
        at = pl.ds(head * width, width)
        scores = jnp.dot(q_ref[:, at], key_ref[...], preferred_element_type=jnp.float32)
        exponent = jnp.exp(scores).astype(jnp.bfloat16)
        both = jnp.dot(exponent, value, preferred_element_type=jnp.float32)
        out_ref[:, at] = both[:, :width].astype(out_ref.dtype)
        total = both[:, width:]
        coarse = total.astype(jnp.bfloat16).astype(jnp.float32)
        packed = jnp.where(lane == head, coarse, packed)
        packed = jnp.where(lane == head + heads, total - coarse, packed)
    out_ref[:, pl.ds(heads * width, width)] = packed.astype(out_ref.dtype)


def attend(queries, keys, values):
    rows, columns = queries.shape
    vmem = pl.BlockSpec(memory_space=pltpu.VMEM)
    return pl.pallas_call(
        attend_kernel,
        in_specs=[vmem] * 3,
        out_specs=vmem,
        out_shape=jax.ShapeDtypeStruct((rows, columns + keys.shape[0]), jnp.bfloat16),
        compiler_params=pltpu.CompilerParams(vmem_limit_bytes=32 << 20),
        name="attend",
    )(queries, keys, values)


def combine_kernel(ids_ref, slots_ref, back_ref, gate_ref, out_ref, table_ref, counts_ref):
    requests, images = ids_ref.shape
    words = out_ref.shape[0] // requests
    columns = out_ref.shape[1]
    width = back_ref.shape[1] - columns
    heads = columns // width

    def visit(request, which, slot):
        table_ref[request * images + which] = slot

    place_requests(ids_ref, slots_ref, counts_ref, visit)
    gate = jnp.tanh(jnp.broadcast_to(gate_ref[...], (words, width)))
    for request in range(0, requests, 2):
        results = []
        for i in range(2):
            slots = [table_ref[(request + i) * images + which] for which in range(images)]
            parts = [
                back_ref[pl.ds(pl.multiple_of(slot * words, words), words)].astype(jnp.float32)
                for slot in slots
            ]
            both = parts[0] + parts[1]
            columns_of = []
            for head in range(heads):
                low = columns + head
                total = both[:, low : low + 1] + both[:, low + heads : low + heads + 1]
                at = slice(head * width, (head + 1) * width)
                columns_of.append(gate * (both[:, at] / total))
            results.append(jnp.concatenate(columns_of, axis=1))
        out_ref[pl.ds(request * words, 2 * words)] = jnp.concatenate(results).astype(out_ref.dtype)


def combine(image_ids, image_slot, back, gate, rows):
    smem = pl.BlockSpec(memory_space=pltpu.SMEM)
    vmem = pl.BlockSpec(memory_space=pltpu.VMEM)
    width = gate.shape[1]
    return pl.pallas_call(
        combine_kernel,
        in_specs=[smem, smem, vmem, vmem],
        out_specs=vmem,
        out_shape=jax.ShapeDtypeStruct((rows, back.shape[1] - width), jnp.bfloat16),
        scratch_shapes=[
            pltpu.SMEM((image_ids.size,), jnp.int32),
            pltpu.SMEM(image_slot.shape, jnp.int32),
        ],
        compiler_params=pltpu.CompilerParams(vmem_limit_bytes=8 << 20),
        name="combine",
    )(image_ids, image_slot, back, gate)


def per_device(
    text_rows, q_weight, features, kv_weight, q_gain, k_gain, attn_gate, image_ids, image_slot
):
    rows = text_rows.shape[0]
    words = rows // image_ids.shape[0]
    images = image_slot.shape[0]
    width = q_gain.shape[0]
    columns = q_weight.shape[1]

    mine = lax.axis_index("feat").astype(jnp.int32).reshape(1)
    kv_weight = pltpu.with_memory_space_constraint(kv_weight, pltpu.HBM)
    q_weight = pltpu.with_memory_space_constraint(q_weight, pltpu.HBM)

    beside = permute(text_rows, 1, 0)

    vision = pltpu.with_memory_space_constraint(features[0].T, pltpu.HBM)
    (key_away,) = project(mine, kv_weight, vision, width, [(1, 0, jnp.float32)], 1)
    key_away = (key_away * KEY_SCALE).astype(jnp.float16)
    key_away = permute(key_away, 1, 0)

    both_texts = jnp.stack([text_rows, beside])
    before = permute(both_texts, 0, 1)
    behind = permute(both_texts, 0, RING - 1)

    queries = query_step(mine, [(0, 0), (1, 0)], [both_texts], q_weight)
    mine, queries = lax.optimization_barrier((mine, queries))
    value_away, key_home, value_home = project(
        mine,
        kv_weight,
        vision,
        width,
        [(1, 1, jnp.bfloat16), (0, 0, jnp.float32), (0, 1, jnp.float32)],
        2,
        pltpu.HBM,
    )
    before, value_away = lax.optimization_barrier((before, value_away))
    around = [permute(before[:1], 0, 1), permute(behind[1:], 0, RING - 1)]
    value_away = permute(value_away, 1, 0)
    places = [(0, -1), (1, -1), (0, 1), (1, 1)]
    queries = query_step(mine, places, [before, behind], q_weight, queries)
    key_away, queries = lax.optimization_barrier((key_away, queries))
    sent = query_last(
        mine, [(0, 2), (1, 2)], image_ids, image_slot, around, q_weight, queries, q_gain
    )
    sent, key_away = lax.optimization_barrier((sent, key_away))
    arrived = lax.all_to_all(
        sent.reshape(images, CAP * words, columns), "dp", 0, 0, tiled=True
    ).reshape(images * CAP * words, columns)

    def finish(home, away, wire, scale):
        def pair(step):
            return home[step] * scale + away[step].astype(jnp.float32)

        passed = [permute(pair(step).astype(wire), 0, step) for step in (1, 3, 2)]
        return functools.reduce(lambda t, p: t + p.astype(jnp.float32), passed, pair(0))

    key = finish(key_home, key_away, jnp.float16, KEY_SCALE)
    key = (
        key
        * lax.rsqrt(jnp.mean(key * key, axis=0, keepdims=True) + epsilon * KEY_SCALE**2)
        * k_gain[:, None]
    )
    key = key.astype(jnp.bfloat16)
    value = finish(value_home, value_away, jnp.bfloat16, 1.0).astype(jnp.bfloat16)

    back = attend(arrived, key, value)
    back = lax.all_to_all(
        back.reshape(images, CAP * words, columns + width), "dp", 0, 0, tiled=True
    ).reshape(images * CAP * words, columns + width)
    gate = jnp.broadcast_to(attn_gate[None], (1, width))
    return combine(image_ids, image_slot, back, gate, rows)


def solution(mesh):
    in_specs = (
        P("dp", "feat"),
        P(None, "feat"),
        P("dp", None, "feat"),
        P("feat", None),
        P(),
        P(),
        P(),
        P("dp", None),
        P(),
    )
    return jax.shard_map(
        per_device, mesh=mesh, in_specs=in_specs, out_specs=P("dp", "feat"), check_vma=False
    )
```
